256 devices in a mesh: mix: 4 (over z_hi), fsdp: 4 (over x), tile: 16 (over z_lo, y, core).
Axes of the slice: x: 4, y: 4, z: 8 (z_hi: 4, z_lo: 2; z = z_hi * 2 + z_lo), core: 2. Of those that a mesh axis runs over, the one named last changes fastest.
Arguments:
- video: bfloat16 [16, 64, 8, 8, 256], P(('mix', 'fsdp'), 'tile'), parts along dimension 0
- conv_weight: bfloat16 [1024, 6912], P(('mix', 'fsdp')), parts along dimension 0, may hold values from -0.078125 to 0.078125
- down_weight: bfloat16 [1024, 2304], P(('mix', 'fsdp')), parts along dimension 0, may hold values from -0.125 to 0.125
- out_grad: bfloat16 [16, 64, 4, 4, 256], P(('mix', 'fsdp'), 'tile'), parts along dimension 0, may hold values from -6 to 6
- clip_bucket: int32 [16], P(('mix', 'fsdp')), parts along dimension 0, may hold values from 0 to 3
- start_frame: int32 [16], P(('mix', 'fsdp')), parts along dimension 0, may hold values from 0 to 32
- bucket_res: int32 [4, 2], replicated, may hold values from 4 to 8, as said below
Outputs:
- down: bfloat16 [16, 64, 4, 4, 256], P(('mix', 'fsdp'), 'tile'), parts along dimension 0
- video_grad: bfloat16 [16, 64, 8, 8, 256], P(('mix', 'fsdp'), 'tile'), parts along dimension 0
- conv_weight_grad: float32 [1024, 6912], P(('mix', 'fsdp')), parts along dimension 0
- down_weight_grad: float32 [1024, 2304], P(('mix', 'fsdp')), parts along dimension 0
The draws below stay inside these ranges and needn't reach their ends.
There are 4 independent parts, one for each index of `mix`. The reference program is written for one: setup_inputs(seed, part) draws one part's arguments, and reference() takes and returns one part's arrays. A program takes and returns all parts, laid end to end along the dimension named above; an argument that names none is the same for every part. Nothing has to cross between parts.
Inputs may be any that keep to these rules, and one draw needn't show every extreme that they name: `start_frame`: frames before it are padding. `bucket_res`: valid rows (column 0) and columns (column 1) per bucket; no two buckets have the same pair.
All inputs are finite; a program needn't handle non-finite values.
Results may differ from the reference program's by a relative error of at most 0.0051.
Values may be sent and summed in bfloat16 or wider, within the bound.
No kernel may reach another device: no remote copies, remote signals or barrier semaphores. Data moves between devices by JAX's collectives and lax.ppermute only.
A program may use at most 128 MiB of HBM per device.

```python
import jax
import jax.numpy as jnp
from jax import lax

CHANNELS = 256
GROUPS = 32
SIDE = 8
BUCKETS = 4
CLIPS = 4
FRAMES = 64


def draw_video(key, part):
    noise_key = jax.random.fold_in(key, 11)
    channel_key = jax.random.fold_in(key, 12)
    full_shape = (CLIPS, FRAMES, SIDE, SIDE, CHANNELS)
    frame_pos = jnp.arange(FRAMES, dtype=jnp.float32) / max(FRAMES - 1, 1)
    channel_scale = jnp.exp(jax.random.uniform(channel_key, (CHANNELS,), jnp.float32, jnp.log(0.3), jnp.log(3.0)))
    noise = jnp.clip(jax.random.normal(noise_key, full_shape, jnp.float32), -5.0, 5.0)
    growth = 1.0 + 2.0 * frame_pos
    return (noise * growth[None, :, None, None, None] * channel_scale).astype(jnp.bfloat16)


def draw_bucket_res(key, part):
    order_key = jax.random.fold_in(key, 21)
    ranks = jax.random.permutation(order_key, jnp.arange(BUCKETS, dtype=jnp.int32))
    half_side = SIDE // 2
    rows = SIDE - ranks * half_side // (BUCKETS - 1)
    cols = SIDE - (BUCKETS - 1 - ranks) * half_side // (BUCKETS - 1)
    return jnp.stack([rows, cols], axis=1).astype(jnp.int32)


def plant(drawn, stream_key, smallest, high):
    shape = drawn.shape
    spot = [jax.random.randint(jax.random.fold_in(stream_key, axis), (), 0, shape[axis]) for axis in range(len(shape))]
    drawn = drawn.at[tuple(spot)].set(smallest)
    longest = shape.index(max(shape))
    spot[longest] = (spot[longest] + 1) % shape[longest]
    return drawn.at[tuple(spot)].set(high)


def with_spikes(array, key, source, target, blocks, factor):
    def block_of(dim):
        return (jnp.arange(array.shape[dim]) // (array.shape[dim] // blocks)).reshape((-1,) + (1,) * (array.ndim - 1 - dim))

    one_side = jax.random.permutation(key, blocks)[block_of(target)]
    far = (block_of(target) + blocks // 2) % blocks
    return jnp.where((block_of(source) == one_side) | (block_of(source) == far), factor * array, array)


def block_levels(stream_key, shape, cuts, least, high):
    factor_of = 1.0
    for dim, blocks in cuts:
        draws = jax.random.uniform(jax.random.fold_in(jax.random.fold_in(stream_key, 6), dim), (blocks,), jnp.float32, least / len(cuts), high / len(cuts))
        factor_of = factor_of * jnp.repeat(jnp.exp(draws), shape[dim] // blocks).reshape((-1,) + (1,) * (len(shape) - 1 - dim))
    return factor_of


def scatter_about(own_key, extent, width, reach, shards=(), held_as=jnp.bfloat16):
    drawn = width * jax.random.normal(own_key, extent, jnp.float32)
    if shards:
        drawn = drawn * block_levels(own_key, extent, shards, -0.22, 0.18)
    return jnp.clip(drawn, -reach, reach).astype(held_as)


def bell_draw_with(rng, dims, scale, reach, split, heavy, kind=jnp.bfloat16):
    array = scale * jax.random.normal(rng, dims, jnp.float32)
    if split:
        array = array * block_levels(rng, dims, split, -0.22, 0.18)
    return jnp.clip(with_spikes(array, jax.random.fold_in(rng, 3), *heavy), -reach, reach).astype(kind)


def setup_inputs(seed: int = 0, part: int = 0) -> dict:
    key_list = jax.random.split(jax.random.key(seed), 8)
    own_keys = jax.random.split(jax.random.fold_in(key_list[7], part), 8)
    video = draw_video(jax.random.fold_in(jax.random.fold_in(key_list[7], part), 71), part)
    conv_weight = scatter_about(own_keys[1], (CHANNELS, 27 * CHANNELS), (27 * CHANNELS) ** -0.5, 0.078125, ((0, 4),))
    down_weight = scatter_about(own_keys[2], (CHANNELS, 9 * CHANNELS), (9 * CHANNELS) ** -0.5, 0.125, ((0, 4),))
    out_grad = bell_draw_with(own_keys[3], (CLIPS, FRAMES, SIDE // 2, SIDE // 2, CHANNELS), 1.0, 6.0, ((0, 4), (1, 16)), (1, 4, 16, 2.0))
    clip_bucket = plant(jax.random.randint(own_keys[4], (CLIPS,), 0, BUCKETS), jax.random.fold_in(own_keys[4], 1), 0, BUCKETS - 1).astype(jnp.int32)
    start_frame = plant(jax.random.randint(own_keys[5], (CLIPS,), 0, FRAMES // 2 + 1), jax.random.fold_in(own_keys[5], 1), 0, (FRAMES // 2 + 1) - 1).astype(jnp.int32)
    bucket_res = draw_bucket_res(jax.random.fold_in(key_list[7], 71), part)
    return dict(video=video, conv_weight=conv_weight, down_weight=down_weight, out_grad=out_grad, clip_bucket=clip_bucket, start_frame=start_frame, bucket_res=bucket_res)


EPSILON = 1e-06

def tap_window(padded, tap_index, out_frames, side_cells, flipped):
    tap_time = tap_index // 9
    tap_row = tap_index // 3 % 3
    tap_col = tap_index % 3
    if flipped:
        tap_time, tap_row, tap_col = (2 - tap_time, 2 - tap_row, 2 - tap_col)
    window = padded[:, tap_time:tap_time + out_frames, tap_row:tap_row + side_cells, tap_col:tap_col + side_cells, :]
    return window.reshape(-1, padded.shape[-1])

def reference(video, conv_weight, down_weight, out_grad, clip_bucket, start_frame, bucket_res):
    channel_count = video.shape[-1]
    group_width = channel_count // GROUPS
    half_side = SIDE // 2
    limits = bucket_res[clip_bucket]
    frame_ids = jnp.arange(FRAMES, dtype=jnp.int32)
    positions = jnp.arange(SIDE, dtype=jnp.int32)
    in_time = frame_ids[None, :] >= start_frame[:, None]
    in_rows = positions[None, :] < limits[:, 0:1]
    in_cols = positions[None, :] < limits[:, 1:2]
    inside = in_time[:, :, None, None] & in_rows[:, None, :, None] & in_cols[:, None, None, :]
    mask = inside.astype(jnp.float32)[..., None]
    valid_count = lax.optimization_barrier(jnp.sum(mask, axis=(1, 2, 3, 4))) * group_width
    grouped_shape = (CLIPS, FRAMES, SIDE, SIDE, GROUPS, group_width)
    summed_axes = (1, 2, 3, 5)
    cell_weight = mask[..., None]
    grouped = video.astype(jnp.float32).reshape(grouped_shape)
    centre = lax.optimization_barrier(jnp.sum(grouped * cell_weight, axis=summed_axes)) / valid_count[:, None]
    offset = grouped - centre[:, None, None, None, :, None]
    spread = lax.optimization_barrier(jnp.sum(cell_weight * offset * offset, axis=summed_axes)) / valid_count[:, None]
    inverse = lax.rsqrt(spread + EPSILON)
    normed_grouped = offset * inverse[:, None, None, None, :, None]
    normed = normed_grouped.reshape(video.shape)
    hidden = (mask * jax.nn.silu(normed)).astype(jnp.bfloat16)
    padded = jnp.pad(hidden, ((0, 0), (2, 0), (1, 1), (1, 1), (0, 0)))
    conv_out = jnp.zeros((CLIPS * FRAMES * SIDE * SIDE, channel_count), jnp.float32)
    for tap_index in range(27):
        window = tap_window(padded, tap_index, FRAMES, SIDE, False)
        panel = conv_weight[:, tap_index * channel_count:(tap_index + 1) * channel_count]
        conv_out = conv_out + lax.dot_general(window, panel, (((1,), (1,)), ((), ())), preferred_element_type=jnp.float32)
    residual = (mask * (video.astype(jnp.float32) + conv_out.reshape(video.shape))).astype(jnp.bfloat16)
    down_padded = jnp.pad(residual, ((0, 0), (0, 0), (0, 1), (0, 1), (0, 0)))
    grad_flat = out_grad.reshape(-1, channel_count)
    down_out = jnp.zeros((CLIPS * FRAMES * half_side * half_side, channel_count), jnp.float32)
    spread_back = jnp.zeros((CLIPS, FRAMES, SIDE + 1, SIDE + 1, channel_count), jnp.float32)
    down_terms = []
    for tap_row in range(3):
        for tap_col in range(3):
            tap_index = tap_row * 3 + tap_col
            panel = down_weight[:, tap_index * channel_count:(tap_index + 1) * channel_count]
            window = down_padded[:, :, tap_row:tap_row + SIDE:2, tap_col:tap_col + SIDE:2, :].reshape(-1, channel_count)
            down_out = down_out + lax.dot_general(window, panel, (((1,), (1,)), ((), ())), preferred_element_type=jnp.float32)
            term = jnp.dot(grad_flat, panel, preferred_element_type=jnp.float32)
            spread_back = spread_back.at[:, :, tap_row:tap_row + SIDE:2, tap_col:tap_col + SIDE:2, :].add(term.reshape(CLIPS, FRAMES, half_side, half_side, channel_count))
            down_terms.append(lax.dot_general(grad_flat, window, (((0,), (0,)), ((), ())), preferred_element_type=jnp.float32))
    down = down_out.reshape(CLIPS, FRAMES, half_side, half_side, channel_count).astype(jnp.bfloat16)
    down_weight_grad = jnp.concatenate(down_terms, axis=1)
    res_grad = (mask * spread_back[:, :, :SIDE, :SIDE, :]).astype(jnp.bfloat16)
    res_flat = res_grad.reshape(-1, channel_count)
    grad_padded = jnp.pad(res_grad, ((0, 0), (0, 2), (1, 1), (1, 1), (0, 0)))
    back_hidden = jnp.zeros((CLIPS * FRAMES * SIDE * SIDE, channel_count), jnp.float32)
    conv_terms = []
    for tap_index in range(27):
        panel = conv_weight[:, tap_index * channel_count:(tap_index + 1) * channel_count]
        window = tap_window(padded, tap_index, FRAMES, SIDE, False)
        conv_terms.append(lax.dot_general(res_flat, window, (((0,), (0,)), ((), ())), preferred_element_type=jnp.float32))
        flipped_window = tap_window(grad_padded, tap_index, FRAMES, SIDE, True)
        back_hidden = back_hidden + jnp.dot(flipped_window, panel, preferred_element_type=jnp.float32)
    conv_weight_grad = jnp.concatenate(conv_terms, axis=1)
    gate_value = jax.nn.sigmoid(normed)
    pushed = mask * back_hidden.reshape(video.shape) * gate_value * (1.0 + normed * (1.0 - gate_value))
    pushed_grouped = pushed.reshape(grouped_shape)
    mean_push = lax.optimization_barrier(jnp.sum(pushed_grouped, axis=summed_axes)) / valid_count[:, None]
    mean_pair = lax.optimization_barrier(jnp.sum(pushed_grouped * normed_grouped, axis=summed_axes)) / valid_count[:, None]
    through_norm = inverse[:, None, None, None, :, None] * (pushed_grouped - mean_push[:, None, None, None, :, None] - normed_grouped * mean_pair[:, None, None, None, :, None])
    video_grad = (mask * through_norm.reshape(video.shape) + res_grad.astype(jnp.float32)).astype(jnp.bfloat16)
    return (down, video_grad, conv_weight_grad, down_weight_grad)
```

```python
import jax
import jax.numpy as jnp
from jax import lax
from jax.sharding import PartitionSpec as P

GROUPS = 32


EPSILON = 1e-06


def shifted(block, axis, distance):
    devices = range(lax.axis_size(axis))
    route = [(i - distance, i) for i in devices if i - distance in devices]
    return lax.ppermute(block, axis, route)


def everywhere(block, axis):
    copies = jnp.broadcast_to(block[None], (lax.axis_size(axis),) + block.shape)
    return lax.all_to_all(copies, axis, 0, 0, tiled=True)


def valid_mask(clip_bucket, start_frame, bucket_res, first_frame, frame_count, side_cells):
    bucket_ids = jnp.arange(bucket_res.shape[0], dtype=jnp.int32)
    picked = (clip_bucket[:, None] == bucket_ids[None, :]).astype(jnp.int32)
    limits = jnp.sum(picked[:, :, None] * bucket_res[None, :, :], axis=1)
    frame_ids = first_frame + jnp.arange(frame_count, dtype=jnp.int32)
    positions = jnp.arange(side_cells, dtype=jnp.int32)
    in_time = frame_ids[None, :] >= start_frame[:, None]
    in_rows = positions[None, :] < limits[:, 0:1]
    in_cols = positions[None, :] < limits[:, 1:2]
    inside = in_time[:, :, None, None] & in_rows[:, None, :, None] & in_cols[:, None, None, :]
    return (inside.astype(jnp.float32)[..., None], limits)


def time_group(padded, tap_time, out_frames, side_cells, flipped):
    channel_count = padded.shape[-1]
    time_start = 2 - tap_time if flipped else tap_time
    layers = []
    for tap_row in range(3):
        for tap_col in range(3):
            row_start = 2 - tap_row if flipped else tap_row
            col_start = 2 - tap_col if flipped else tap_col
            window = padded[
                :,
                time_start : time_start + out_frames,
                row_start : row_start + side_cells,
                col_start : col_start + side_cells,
                :,
            ]
            layers.append(window.reshape(-1, channel_count))
    return jnp.stack(layers)


def stride_taps(padded, side_cells):
    channel_count = padded.shape[-1]
    layers = []
    for tap_row in range(3):
        for tap_col in range(3):
            window = padded[
                :, :, tap_row : tap_row + side_cells : 2, tap_col : tap_col + side_cells : 2, :
            ]
            layers.append(window.reshape(-1, channel_count))
    return jnp.stack(layers)


def weight_terms(grad_rows, slabs, cot_rows, hidden_padded, frame_count, side_cells):
    out_rows = grad_rows.shape[1]
    down_term = lax.dot_general(
        grad_rows, slabs, (((0,), (1,)), ((), ())), preferred_element_type=jnp.float32
    ).reshape(out_rows, -1)
    conv_parts = []
    for tap_time in range(3):
        group = time_group(hidden_padded, tap_time, frame_count, side_cells, False)
        conv_parts.append(
            lax.dot_general(
                cot_rows, group, (((0,), (1,)), ((), ())), preferred_element_type=jnp.float32
            )
        )
    conv_term = jnp.concatenate(conv_parts, axis=1).reshape(out_rows, -1)
    return (conv_term, down_term)


def transpose_conv(grad_padded, conv_weight, out_frames, side_cells):
    channel_count = grad_padded.shape[-1]
    row_total = grad_padded.shape[0] * out_frames * side_cells * side_cells
    initial = jnp.zeros((row_total, channel_count), jnp.float32)
    running = initial
    weight_panel = lax.all_gather(conv_weight, "fsdp", axis=0, tiled=True)
    panel_rows = weight_panel.shape[0]
    panel = weight_panel.reshape(panel_rows, 27, channel_count)
    for tap_time in range(3):
        group = time_group(grad_padded, tap_time, out_frames, side_cells, True)
        running = running + lax.dot_general(
            group,
            panel[:, 9 * tap_time : 9 * tap_time + 9, :],
            (((0, 2), (1, 0)), ((), ())),
            preferred_element_type=jnp.float32,
        )
    return running


def shards(video, conv_weight, down_weight, out_grad, clip_bucket, start_frame, bucket_res):
    clip_count, frame_count, side_cells, side_again, channel_count = video.shape
    half_side = side_cells // 2
    group_width = channel_count // GROUPS
    tiles = lax.axis_size("tile")
    mask, limits = valid_mask(
        clip_bucket,
        start_frame,
        bucket_res,
        lax.axis_index("tile") * frame_count,
        frame_count,
        side_cells,
    )
    valid_count = (
        (frame_count * tiles - start_frame) * limits[:, 0] * limits[:, 1] * group_width
    ).astype(jnp.float32)
    grouped_shape = (clip_count, frame_count, side_cells, side_cells, GROUPS, group_width)
    summed_axes = (1, 2, 3, 5)
    cell_weight = mask[..., None]
    grouped = video.astype(jnp.float32).reshape(grouped_shape)
    cells_per_frame = limits[:, 0] * limits[:, 1] * group_width
    tile_starts = jnp.arange(tiles, dtype=jnp.int32)[:, None] * frame_count
    tile_frames = jnp.clip(tile_starts + frame_count - start_frame[None, :], 0, frame_count)
    tile_counts = (tile_frames * cells_per_frame[None, :]).astype(jnp.float32)[:, :, None]
    own_count = jnp.sum(mask, axis=(1, 2, 3, 4))[:, None] * group_width
    own_sum = jnp.sum(grouped * cell_weight, axis=summed_axes)
    own_mean = own_sum / jnp.maximum(own_count, 1.0)
    own_offset = grouped - own_mean[:, None, None, None, :, None]
    own_square = jnp.sum(cell_weight * own_offset * own_offset, axis=summed_axes)
    stats = everywhere(jnp.stack([own_sum, own_square]), "tile")
    tile_sums = stats[:, 0]
    centre = jnp.sum(tile_sums, axis=0) / valid_count[:, None]
    tile_drift = tile_sums / jnp.maximum(tile_counts, 1.0) - centre[None]
    second_sum = jnp.sum(stats[:, 1] + tile_counts * tile_drift * tile_drift, axis=0)
    spread = second_sum / valid_count[:, None]
    offset = grouped - centre[:, None, None, None, :, None]
    inverse = lax.rsqrt(spread + EPSILON)
    normed_grouped = offset * inverse[:, None, None, None, :, None]
    normed = normed_grouped.reshape(video.shape)
    hidden = (mask * jax.nn.silu(normed)).astype(jnp.bfloat16)
    past = shifted(hidden[:, frame_count - 2 :], "tile", 1)
    hidden_padded = jnp.pad(
        jnp.concatenate([past, hidden], axis=1), ((0, 0), (0, 0), (1, 1), (1, 1), (0, 0))
    )

    def conv_columns(weight_panel):
        panel = weight_panel.reshape(weight_panel.shape[0], 27, channel_count)
        summed = None
        for tap_time in range(3):
            group = time_group(hidden_padded, tap_time, frame_count, side_cells, False)
            term = lax.dot_general(
                group,
                panel[:, 9 * tap_time : 9 * tap_time + 9, :],
                (((0, 2), (1, 2)), ((), ())),
                preferred_element_type=jnp.float32,
            )
            summed = term if summed is None else summed + term
        return summed

    conv_out = conv_columns(lax.all_gather(conv_weight, "fsdp", axis=0, tiled=True))
    residual = (mask * (video.astype(jnp.float32) + conv_out.reshape(video.shape))).astype(
        jnp.bfloat16
    )
    down_slabs = stride_taps(
        jnp.pad(residual, ((0, 0), (0, 0), (0, 1), (0, 1), (0, 0))), side_cells
    )
    weight_panel = lax.all_gather(down_weight, "fsdp", axis=0, tiled=True)
    panel = weight_panel.reshape(weight_panel.shape[0], 9, channel_count)
    down_out = lax.dot_general(
        down_slabs, panel, (((0, 2), (1, 2)), ((), ())), preferred_element_type=jnp.float32
    )
    down = down_out.astype(jnp.bfloat16).reshape(
        clip_count, frame_count, half_side, half_side, channel_count
    )
    grad_flat = out_grad.reshape(-1, channel_count)
    weight_panel = lax.all_gather(down_weight, "fsdp", axis=0, tiled=True)
    panel_rows = weight_panel.shape[0]
    panel = weight_panel.reshape(panel_rows, 9, channel_count)
    tap_grads = lax.dot_general(
        grad_flat, panel, (((1,), (0,)), ((), ())), preferred_element_type=jnp.float32
    )
    spread_back = jnp.zeros(
        (clip_count, frame_count, side_cells + 1, side_cells + 1, channel_count), jnp.float32
    )
    for tap_row in range(3):
        for tap_col in range(3):
            term = tap_grads[:, tap_row * 3 + tap_col, :].reshape(
                clip_count, frame_count, half_side, half_side, channel_count
            )
            spread_back = spread_back.at[
                :, :, tap_row : tap_row + side_cells : 2, tap_col : tap_col + side_cells : 2, :
            ].add(term)
    res_grad = (mask * spread_back[:, :, :side_cells, :side_cells, :]).astype(jnp.bfloat16)
    res_flat = res_grad.reshape(-1, channel_count)
    later = shifted(res_grad[:, :2], "tile", -1)
    grad_padded = jnp.pad(
        jnp.concatenate([res_grad, later], axis=1), ((0, 0), (0, 0), (1, 1), (1, 1), (0, 0))
    )
    back_hidden = transpose_conv(grad_padded, conv_weight, frame_count, side_cells).reshape(
        video.shape
    )
    gate_value = jax.nn.sigmoid(normed)
    pushed = mask * back_hidden * gate_value * (1.0 + normed * (1.0 - gate_value))
    pushed_grouped = pushed.reshape(grouped_shape)
    pushes = everywhere(
        jnp.stack(
            [
                jnp.sum(pushed_grouped, axis=summed_axes),
                jnp.sum(pushed_grouped * normed_grouped, axis=summed_axes),
            ]
        ),
        "tile",
    )
    push_sum, pair_sum = jnp.sum(pushes, axis=0)
    mean_push = push_sum / valid_count[:, None]
    mean_pair = pair_sum / valid_count[:, None]
    through_norm = inverse[:, None, None, None, :, None] * (
        pushed_grouped
        - mean_push[:, None, None, None, :, None]
        - normed_grouped * mean_pair[:, None, None, None, :, None]
    )
    video_grad = (mask * through_norm.reshape(video.shape) + res_grad.astype(jnp.float32)).astype(
        jnp.bfloat16
    )
    parts = lax.axis_size("fsdp") * tiles
    conv_term, down_term = weight_terms(
        grad_flat, down_slabs, res_flat, hidden_padded, frame_count, side_cells
    )
    conv_width = conv_term.shape[1]
    terms = jnp.concatenate([conv_term, down_term], axis=1).astype(jnp.bfloat16)
    terms = terms.reshape(parts, -1, terms.shape[1])
    exchanged = lax.all_to_all(terms, ("fsdp", "tile"), 0, 0, tiled=True)
    share = jnp.sum(exchanged.astype(jnp.float32), axis=0).astype(jnp.bfloat16)
    rows = lax.all_gather(share, "tile", axis=0, tiled=True)
    conv_weight_grad = rows[:, :conv_width].astype(jnp.float32)
    down_weight_grad = rows[:, conv_width:].astype(jnp.float32)
    return (down, video_grad, conv_weight_grad, down_weight_grad)


def solution(mesh):
    placed = (
        P(("mix", "fsdp"), "tile", None, None, None),
        P(("mix", "fsdp"), None),
        P(("mix", "fsdp"), None),
        P(("mix", "fsdp"), "tile", None, None, None),
        P(("mix", "fsdp")),
        P(("mix", "fsdp")),
        P(),
    )
    return jax.shard_map(
        shards,
        mesh=mesh,
        in_specs=placed,
        out_specs=(
            P(("mix", "fsdp"), "tile", None, None, None),
            P(("mix", "fsdp"), "tile", None, None, None),
            P(("mix", "fsdp"), None),
            P(("mix", "fsdp"), None),
        ),
        check_vma=False,
    )
```
